256 devices in a mesh: seq: 32 (over x, z_lo, core), head: 8 (over z_hi, y).
Axes of the slice: x: 4, y: 4, z: 8 (z_hi: 2, z_lo: 4; z = z_hi * 4 + z_lo), core: 2. Of those that a mesh axis runs over, the one named last changes fastest.
Arguments:
- normed: bfloat16 [16384, 5376], P('seq'), may hold values from -6 to 6
- cotangent: bfloat16 [16384, 2048], P('seq', 'head'), may hold values from -6 to 6
- qkv_master: float32 [5376, 8, 512], P('seq', 'head'), may hold values from -0.078125 to 0.078125
- adam_first: float32 [5376, 8, 512], P('seq', 'head'), may hold values from -6 to 6
- adam_second: float32 [5376, 8, 512], P('seq', 'head'), may hold values from 0.5 to 20
- skip_flag: int32 [8], replicated, may hold values 0 or 1
- scale_exponent: int32 [1], replicated, may hold values from 4 to 8
Outputs:
- attn_out: bfloat16 [16384, 2048], P('seq', 'head')
- d_tokens: bfloat16 [16384, 5376], P(('seq', 'head'))
- new_master: float32 [5376, 8, 512], P('seq', 'head')
- new_first: float32 [5376, 8, 512], P('seq', 'head')
- new_second: float32 [5376, 8, 512], P('seq', 'head')
The draws below stay inside these ranges and needn't reach their ends.
All inputs are finite; a program needn't handle non-finite values.
Results may differ from the reference program's by a relative error of at most 0.0095.
Values may be sent and summed in bfloat16 or wider, within the bound.
No kernel may reach another device: no remote copies, remote signals or barrier semaphores. Data moves between devices by JAX's collectives and lax.ppermute only.
A program may use at most 128 MiB of HBM per device.

```python
import math
import jax
import jax.numpy as jnp
from jax import lax

D = 5376
HEAD_DIM = 128
ATTEND_SPAN = 1024
ATTN_SCALAR = 168
KV_HEADS = 8
Q_PER_KV = 2
ADAM_STEP = 1000
TOK_DEV = 512
TOKENS = 16384
Q_HEADS = 16
GROUP_COLS = 512


def set_ends(entries, own_key, low, largest):
    shape = entries.shape
    spot = [jax.random.randint(jax.random.fold_in(own_key, axis), (), 0, shape[axis]) for axis in range(len(shape))]
    entries = entries.at[tuple(spot)].set(low)
    longest = shape.index(max(shape))
    spot[longest] = (spot[longest] + 1) % shape[longest]
    return entries.at[tuple(spot)].set(largest)


def strengthened(drawn, key, source, target, shards_of, factor):
    def block_of(axis_at):
        return (jnp.arange(drawn.shape[axis_at]) // (drawn.shape[axis_at] // shards_of)).reshape((-1,) + (1,) * (drawn.ndim - 1 - axis_at))

    one_side = jax.random.permutation(key, shards_of)[block_of(target)]
    far = (block_of(target) + shards_of // 2) % shards_of
    return jnp.where((block_of(source) == one_side) | (block_of(source) == far), factor * drawn, drawn)


def shard_levels(rng, shape, split, least, top_value):
    level = 1.0
    for dim, shards_of in split:
        draws = jax.random.uniform(jax.random.fold_in(jax.random.fold_in(rng, 6), dim), (shards_of,), jnp.float32, least / len(split), top_value / len(split))
        level = level * jnp.repeat(jnp.exp(draws), shape[dim] // shards_of).reshape((-1,) + (1,) * (len(shape) - 1 - dim))
    return level


def normal_values(rng, dims, deviation, most, pieces=(), kind=jnp.bfloat16):
    entries = jax.random.normal(rng, dims, jnp.float32) * deviation
    if len(pieces) > 0:
        entries = shard_levels(rng, dims, pieces, -0.22, 0.18) * entries
    return jnp.clip(entries, min=-most, max=most).astype(kind)


def gaussian_with(key, shape, scale, reach, cuts, heavy, kind=jnp.bfloat16):
    drawn = scale * jax.random.normal(key, shape, jnp.float32)
    if cuts:
        drawn = drawn * shard_levels(key, shape, cuts, -0.22, 0.18)
    return jnp.clip(strengthened(drawn, jax.random.fold_in(key, 3), *heavy), -reach, reach).astype(kind)


def setup_inputs(seed: int = 0) -> dict:
    arg_keys = jax.random.split(jax.random.key(seed), 8)
    normed = gaussian_with(arg_keys[0], (TOKENS, D), 1.0, 6.0, ((0, 32),), (0, 1, 32, 2.75))
    cotangent = normal_values(arg_keys[1], (TOKENS, Q_HEADS * HEAD_DIM), 1.0, 6.0, ((0, 32), (1, 8)))
    qkv_master = normal_values(arg_keys[2], (D, KV_HEADS, GROUP_COLS), D ** -0.5, 0.078125, ((0, 32), (1, 8)), jnp.float32)
    adam_first = normal_values(arg_keys[3], (D, KV_HEADS, GROUP_COLS), 1.0, 6.0, ((0, 32), (1, 8)), jnp.float32)
    adam_second = jnp.clip(jnp.exp(math.log(20.0) - 3.6888795 * jax.random.uniform(arg_keys[4], (D, KV_HEADS, GROUP_COLS), jnp.float32) ** shard_levels(arg_keys[4], (D, KV_HEADS, GROUP_COLS), ((0, 32), (1, 8)), -0.2, 0.2)), 0.5, 20.0)
    skip_flag = set_ends((jax.random.randint(arg_keys[5], (KV_HEADS,), 0, 2) < 1).astype(jnp.int32), jax.random.fold_in(arg_keys[5], 1), 0, 1)
    scale_exponent = jax.random.randint(arg_keys[6], (1,), 4, 9).astype(jnp.int32)
    return {"normed": normed, "cotangent": cotangent, "qkv_master": qkv_master, "adam_first": adam_first, "adam_second": adam_second, "skip_flag": skip_flag, "scale_exponent": scale_exponent}


norm_eps = 1e-06
beta_one = 0.9
beta_two = 0.95
adam_eps = 1e-08
learn_rate = 0.01
weight_decay = 0.1

def head_norm(raw_vals):
    factor = lax.rsqrt(lax.optimization_barrier(jnp.mean(raw_vals * raw_vals, axis=-1, keepdims=True)) + norm_eps)
    return (raw_vals * factor, factor)

def norm_back(raw_vals, factor, grad_in):
    inner_mean = lax.optimization_barrier(jnp.mean(raw_vals * grad_in, axis=-1, keepdims=True))
    return factor * grad_in - raw_vals * factor * factor * factor * inner_mean

def window_kernel(query_tile, key_tile, query_start, key_start):
    score_scale = float(ATTN_SCALAR) ** (-0.5)
    scores = jnp.einsum('tgqd,lgd->gqtl', query_tile.astype(jnp.float32), key_tile.astype(jnp.float32)) * score_scale
    query_pos = query_start + jnp.arange(query_tile.shape[0], dtype=jnp.int32)
    key_pos = key_start + jnp.arange(key_tile.shape[0], dtype=jnp.int32)
    gap_len = query_pos[:, None] - key_pos[None, :]
    allowed = (key_pos[None, :] >= 0) & (gap_len >= 0) & (gap_len < ATTEND_SPAN)
    return jnp.where(allowed, jnp.exp(scores), 0.0)

def reference(normed, cotangent, qkv_master, adam_first, adam_second, skip_flag, scale_exponent):
    total_rows = normed.shape[0]
    model_width = normed.shape[1]
    q_cols = Q_PER_KV * HEAD_DIM
    score_scale = float(ATTN_SCALAR) ** (-0.5)
    master16 = qkv_master.astype(jnp.bfloat16)
    flat16 = master16.reshape(model_width, KV_HEADS * GROUP_COLS)
    qkv = jnp.dot(normed, flat16, preferred_element_type=jnp.float32).reshape(total_rows, KV_HEADS, GROUP_COLS)
    q_raw = qkv[:, :, :q_cols].reshape(total_rows, KV_HEADS, Q_PER_KV, HEAD_DIM)
    k_raw = qkv[:, :, q_cols:q_cols + HEAD_DIM]
    v_raw = qkv[:, :, q_cols + HEAD_DIM:]
    q_unit, q_factor = head_norm(q_raw)
    k_unit, k_factor = head_norm(k_raw)
    queries = lax.optimization_barrier(q_unit.astype(jnp.bfloat16))
    key_tiles = lax.optimization_barrier(k_unit.astype(jnp.bfloat16))
    values = lax.optimization_barrier(v_raw.astype(jnp.bfloat16))
    scale_power = jnp.left_shift(jnp.int32(1), scale_exponent[0]).astype(jnp.float32)
    grad_out = lax.optimization_barrier((cotangent.astype(jnp.float32) * scale_power).astype(jnp.bfloat16))
    grad_out = grad_out.reshape(total_rows, KV_HEADS, Q_PER_KV, HEAD_DIM)
    pad_keys = jnp.concatenate([jnp.zeros((ATTEND_SPAN, KV_HEADS, HEAD_DIM), jnp.bfloat16), key_tiles], 0)
    pad_values = jnp.concatenate([jnp.zeros((ATTEND_SPAN, KV_HEADS, HEAD_DIM), jnp.bfloat16), values], 0)
    window_length = TOK_DEV + ATTEND_SPAN

    def single_block(carry_state, block_index):
        padded_key_gradient, padded_value_gradient = carry_state
        starting_row = (block_index * TOK_DEV).astype(jnp.int32)
        q_block = lax.dynamic_slice_in_dim(queries, starting_row, TOK_DEV, 0)
        go_block = lax.dynamic_slice_in_dim(grad_out, starting_row, TOK_DEV, 0)
        k_block = lax.dynamic_slice_in_dim(pad_keys, starting_row, window_length, 0)
        v_block = lax.dynamic_slice_in_dim(pad_values, starting_row, window_length, 0)
        kernel = window_kernel(q_block, k_block, starting_row, starting_row - ATTEND_SPAN)
        totals = lax.optimization_barrier(jnp.sum(kernel, axis=-1, keepdims=True))
        prob_tile = lax.optimization_barrier((kernel / totals).astype(jnp.bfloat16))
        attention_blend = jnp.einsum('gqtl,lgd->tgqd', prob_tile.astype(jnp.float32), v_block.astype(jnp.float32))
        row_delta = jnp.transpose(lax.optimization_barrier(jnp.sum(go_block.astype(jnp.float32) * attention_blend, axis=-1)), (1, 2, 0))
        grad_probs = jnp.einsum('tgqd,lgd->gqtl', go_block.astype(jnp.float32), v_block.astype(jnp.float32))
        grad_scores = (prob_tile.astype(jnp.float32) * (grad_probs - row_delta[..., None]) * score_scale).astype(jnp.bfloat16)
        grad_scores = lax.optimization_barrier(grad_scores).astype(jnp.float32)
        query_gradient = jnp.einsum('gqtl,lgd->tgqd', grad_scores, k_block.astype(jnp.float32))
        grad_k = jnp.einsum('gqtl,tgqd->lgd', grad_scores, q_block.astype(jnp.float32))
        value_gradient = jnp.einsum('gqtl,tgqd->lgd', prob_tile.astype(jnp.float32), go_block.astype(jnp.float32))
        old_k = lax.dynamic_slice_in_dim(padded_key_gradient, starting_row, window_length, 0)
        previous_value = lax.dynamic_slice_in_dim(padded_value_gradient, starting_row, window_length, 0)
        padded_key_gradient = lax.dynamic_update_slice_in_dim(padded_key_gradient, old_k + grad_k, starting_row, 0)
        padded_value_gradient = lax.dynamic_update_slice_in_dim(padded_value_gradient, previous_value + value_gradient, starting_row, 0)
        return ((padded_key_gradient, padded_value_gradient), (attention_blend.astype(jnp.bfloat16), query_gradient))
    zeroed_padding = jnp.zeros((ATTEND_SPAN + total_rows, KV_HEADS, HEAD_DIM), jnp.float32)
    block_numbers = jnp.arange(total_rows // TOK_DEV, dtype=jnp.int32)
    (padded_key_gradient, padded_value_gradient), (output_blocks, query_block_gradients) = lax.scan(single_block, (zeroed_padding, zeroed_padding), block_numbers)
    attn_out = output_blocks.reshape(total_rows, KV_HEADS * Q_PER_KV * HEAD_DIM)
    grad_queries = query_block_gradients.reshape(total_rows, KV_HEADS, Q_PER_KV, HEAD_DIM)
    grad_keys = padded_key_gradient[ATTEND_SPAN:]
    gradient_value_rows = padded_value_gradient[ATTEND_SPAN:]
    grad_qraw = norm_back(q_raw, q_factor, grad_queries)
    grad_kraw = norm_back(k_raw, k_factor, grad_keys)
    grad_qkv = jnp.concatenate([grad_qraw.reshape(total_rows, KV_HEADS, q_cols), grad_kraw, gradient_value_rows], -1).astype(jnp.bfloat16)
    grad_flat = grad_qkv.reshape(total_rows, KV_HEADS * GROUP_COLS)
    d_tokens = jnp.dot(grad_flat, flat16.T, preferred_element_type=jnp.float32).astype(jnp.bfloat16)
    summed = jnp.dot(normed.T, grad_flat, preferred_element_type=jnp.float32)
    gradient = (summed / scale_power).reshape(model_width, KV_HEADS, GROUP_COLS)
    first_new = beta_one * adam_first + (1.0 - beta_one) * gradient
    second_new = beta_two * adam_second + (1.0 - beta_two) * gradient * gradient
    first_fix = 1.0 - beta_one ** ADAM_STEP
    second_fix = 1.0 - beta_two ** ADAM_STEP
    update = first_new / first_fix / (jnp.sqrt(second_new / second_fix) + adam_eps)
    master_new = qkv_master - learn_rate * (update + weight_decay * qkv_master)
    applied = (skip_flag == 0)[None, :, None]
    return (attn_out, d_tokens, jnp.where(applied, master_new, qkv_master), jnp.where(applied, first_new, adam_first), jnp.where(applied, second_new, adam_second))
```

```python
import jax
import jax.numpy as jnp
from jax import lax
from jax.sharding import PartitionSpec as P

HEAD_DIM = 128
ATTEND_SPAN = 1024
ATTN_SCALAR = 168
Q_PER_KV = 2
ADAM_STEP = 1000

norm_eps = 1e-06
beta_one = 0.9
beta_two = 0.95
adam_eps = 1e-08
learn_rate = 0.01
weight_decay = 0.1

bf16 = jnp.bfloat16
f32 = jnp.float32

SEQ = 32
HEAD = 8


def seq_move(block, dx=0, dz=0, swap=False):
    pairs = []
    for s in range(SEQ):
        x, z, c = s // 8, (s // 2) % 4, s % 2
        pairs.append((s, ((x + dx) % 4) * 8 + ((z + dz) % 4) * 2 + (c ^ int(swap))))
    return lax.ppermute(block, "seq", pairs)


def head_move(block, dy=0, flip=False):
    pairs = []
    for h in range(HEAD):
        half, y = h // 4, h % 4
        pairs.append((h, (half ^ int(flip)) * 4 + (y + dy) % 4))
    return lax.ppermute(block, "head", pairs)


def swap_cores(block):
    return seq_move(block, swap=True)


def shifted(block, distance):
    route = [(i - distance, i) for i in range(SEQ) if 0 <= i - distance < SEQ]
    return lax.ppermute(block, "seq", route)


def tie(later, *earlier):
    return lax.optimization_barrier((later,) + earlier)[0]


def place(blocks, spots):
    out = jnp.zeros((4,) + blocks[0].shape, blocks[0].dtype)
    for block, spot in zip(blocks, spots):
        out = lax.dynamic_update_slice(out, block[None], (spot,) + (0,) * block.ndim)
    return out.reshape((-1,) + blocks[0].shape[1:])


def gather_z(block, z):
    parts = [block] + [seq_move(block, dz=k) for k in (1, 2, 3)]
    return place(parts, [(z - k) % 4 for k in range(4)])


def gather_x(block, x):
    half = block.shape[0] // 2
    left = seq_move(block, dx=1)
    right = seq_move(block, dx=-1)
    far_top = seq_move(left[:half], dx=1)
    far_low = seq_move(right[half:], dx=-1)
    far = jnp.concatenate([far_top, far_low], 0)
    return place([block, left, far, right], [x, (x - 1) % 4, (x + 2) % 4, (x + 1) % 4])


def ring_reduce(blocks, pos, move):
    half = blocks.shape[1] // 2
    pick = lambda k: lax.dynamic_index_in_dim(blocks, (pos + k) % 4, 0, keepdims=False)
    own, ahead, far, back = pick(0), pick(1), pick(2), pick(3)
    top = move(far[:half], 1)
    low = move(far[half:], -1)
    ahead = jnp.concatenate(
        [(ahead[:half].astype(f32) + top.astype(f32)).astype(bf16), ahead[half:]], 0
    )
    back = jnp.concatenate(
        [back[:half], (back[half:].astype(f32) + low.astype(f32)).astype(bf16)], 0
    )
    from_back = move(ahead, 1)
    from_ahead = move(back, -1)
    return own.astype(f32) + from_back.astype(f32) + from_ahead.astype(f32)


def reduce_x(total, x):
    return ring_reduce(total.reshape(4, -1, total.shape[1]), x, lambda b, d: seq_move(b, dx=d))


def reduce_z(total, z):
    blocks = total.reshape(4, -1, total.shape[1])
    pick = lambda k: lax.dynamic_index_in_dim(blocks, (z + k) % 4, 0, keepdims=False)
    out = pick(0).astype(f32)
    for k in (1, 2, 3):
        out = out + seq_move(pick(k), dz=k).astype(f32)
    return out


def head_norm(raw_vals):
    factor = lax.rsqrt(jnp.mean(raw_vals * raw_vals, axis=-1, keepdims=True) + norm_eps)
    return (raw_vals * factor, factor)


def norm_back(raw_vals, factor, grad_in):
    inner_mean = jnp.mean(raw_vals * grad_in, axis=-1, keepdims=True)
    return factor * grad_in - raw_vals * factor * factor * factor * inner_mean


def window_kernel(query_tile, key_tile, query_start, key_start):
    score_scale = float(ATTN_SCALAR) ** (-0.5)
    scores = (
        jnp.einsum("tqd,ld->qtl", query_tile, key_tile, preferred_element_type=f32) * score_scale
    )
    query_pos = query_start + jnp.arange(query_tile.shape[0], dtype=jnp.int32)
    key_pos = key_start + jnp.arange(key_tile.shape[0], dtype=jnp.int32)
    gap_len = query_pos[:, None] - key_pos[None, :]
    allowed = (key_pos[None, :] >= 0) & (gap_len >= 0) & (gap_len < ATTEND_SPAN)
    return jnp.where(allowed, jnp.exp(scores), 0.0)


def pair_cols(even, a, b):
    return jnp.where(even, a, b), jnp.where(even, b, a)


def rows_pair(even, mine, theirs):
    return jnp.where(even, jnp.concatenate([mine, theirs], 0), jnp.concatenate([theirs, mine], 0))


def nt(a, b):
    return lax.dot_general(a, b, (((1,), (1,)), ((), ())), preferred_element_type=f32)


def tn(a, b):
    return lax.dot_general(a, b, (((0,), (0,)), ((), ())), preferred_element_type=f32)


def per_device(normed, cotangent, qkv_master, adam_first, adam_second, skip_flag, scale_exponent):
    tok_rows = normed.shape[0]
    hd = HEAD_DIM
    own_rows = qkv_master.shape[0]
    halo_span = ATTEND_SPAN // tok_rows
    score_scale = float(ATTN_SCALAR) ** (-0.5)
    seq_pos = lax.axis_index("seq")
    head_pos = lax.axis_index("head")
    x, z, core = seq_pos // 8, (seq_pos // 2) % 4, seq_pos % 2
    y, half = head_pos % 4, head_pos // 4
    even = core == 0

    master16 = qkv_master.reshape(own_rows, 4 * hd).astype(bf16)
    cols = [master16[:, i * hd : (i + 1) * hd] for i in range(4)]
    kv_mine, kv_theirs = pair_cols(even, cols[2], cols[3])
    q_mine, q_theirs = pair_cols(even, cols[0], cols[1])
    got = swap_cores(jnp.concatenate([kv_theirs, q_theirs], 1))
    kv_block = rows_pair(even, kv_mine, got[:, :hd])
    q_block = rows_pair(even, q_mine, got[:, hd:])
    far_block = head_move(jnp.concatenate([kv_block, q_block], 1), flip=True)

    kv_plane = gather_z(kv_block, z)
    q_plane = gather_z(q_block, z)
    kv_weights = gather_x(kv_plane, x)
    kv_other = swap_cores(kv_weights)
    q_weights = gather_x(q_plane, x)
    q_other = swap_cores(q_weights)
    w_kv = jnp.concatenate([kv_weights, kv_other], 1)
    w_q = jnp.concatenate([q_weights, q_other], 1)

    far_plane = gather_z(tie(far_block, q_plane), z)
    far_weights = gather_x(tie(far_plane, q_weights), x)
    far_other = swap_cores(far_weights)

    kv = jnp.dot(normed, w_kv, preferred_element_type=f32)
    k_raw, v_raw = pair_cols(even, kv[:, :hd], kv[:, hd:])
    k_unit, k_factor = head_norm(k_raw)
    kv16 = jnp.concatenate([k_unit.astype(bf16), v_raw.astype(bf16)], 1)
    ext = jnp.concatenate([shifted(kv16, 2), shifted(kv16, 1), kv16], 0)
    ext_keys, ext_values = ext[:, :hd], ext[:, hd:]

    qm = jnp.dot(normed, w_q, preferred_element_type=f32)
    q_a, q_b = pair_cols(even, qm[:, :hd], qm[:, hd:])
    q_raw = jnp.stack([q_a, q_b], 1)
    q_unit, q_factor = head_norm(q_raw)
    queries = q_unit.astype(bf16)

    query_start = seq_pos * tok_rows
    key_start = query_start - halo_span * tok_rows
    kernel = window_kernel(queries, ext_keys, query_start, key_start)
    totals = jnp.sum(kernel, axis=-1, keepdims=True)
    prob_tile = (kernel / totals).astype(bf16)
    mixed = jnp.einsum("qtl,ld->tqd", prob_tile, ext_values, preferred_element_type=f32)
    attn_out = mixed.astype(bf16).reshape(tok_rows, Q_PER_KV * hd)
    scale_power = jnp.left_shift(jnp.int32(1), scale_exponent[0]).astype(f32)
    grad_out = (cotangent.astype(f32) * scale_power).astype(bf16)
    grad_out = grad_out.reshape(tok_rows, Q_PER_KV, hd)
    row_delta = jnp.transpose(jnp.sum(grad_out.astype(f32) * mixed, axis=-1), (1, 0))
    grad_probs = jnp.einsum("tqd,ld->qtl", grad_out, ext_values, preferred_element_type=f32)
    grad_scores = (
        prob_tile.astype(f32) * (grad_probs - row_delta[..., None]) * score_scale
    ).astype(bf16)
    grad_keys_ext = jnp.einsum("qtl,tqd->ld", grad_scores, queries, preferred_element_type=f32)
    grad_values_ext = jnp.einsum("qtl,tqd->ld", prob_tile, grad_out, preferred_element_type=f32)
    grad_kv = [
        jnp.concatenate(
            [grad_keys_ext[i * tok_rows : (i + 1) * tok_rows],
             grad_values_ext[i * tok_rows : (i + 1) * tok_rows]], 1)
        for i in range(3)
    ]
    back_one = shifted(grad_kv[1].astype(bf16), -1)
    back_two = shifted(grad_kv[0].astype(bf16), -2)
    grad_queries = jnp.einsum("qtl,ld->tqd", grad_scores, ext_keys, preferred_element_type=f32)

    g_q = norm_back(q_raw, q_factor, grad_queries).astype(bf16)
    gq_mine, gq_theirs = pair_cols(even, g_q[:, 0], g_q[:, 1])

    def exchange_half(g):
        own_half = lax.dynamic_slice_in_dim(g, half * (tok_rows // 2), tok_rows // 2, 0)
        far_half = lax.dynamic_slice_in_dim(g, (1 - half) * (tok_rows // 2), tok_rows // 2, 0)
        return own_half, head_move(far_half, flip=True)

    def weight_terms(mine, theirs):
        send = tn(normed, theirs).astype(bf16)
        got = swap_cores(send)
        return (tn(normed, mine) + got.astype(f32)).astype(bf16)

    gq_pair = jnp.concatenate([gq_mine, gq_theirs], 1)
    gq_own, gq_far = exchange_half(gq_pair)
    wq_x = reduce_x(weight_terms(gq_mine, gq_theirs), x).astype(bf16)
    wq_z = reduce_z(wq_x, z)

    grad_kv_sum = grad_kv[2] + back_one.astype(f32) + back_two.astype(f32)
    g_k = norm_back(k_raw, k_factor, grad_kv_sum[:, :hd]).astype(bf16)
    g_v = grad_kv_sum[:, hd:].astype(bf16)
    gkv_mine, gkv_theirs = pair_cols(even, g_k, g_v)
    gkv_own, gkv_far = exchange_half(jnp.concatenate([gkv_mine, gkv_theirs], 1))
    wkv_x = reduce_x(weight_terms(gkv_mine, gkv_theirs), x).astype(bf16)
    wkv_z = reduce_z(wkv_x, z)

    g_all = jnp.concatenate([gkv_own, gq_own, gkv_far, gq_far], 1)
    w_all = jnp.concatenate([w_kv, w_q, far_weights[:, :hd], far_other[:, :hd],
                             far_weights[:, hd:], far_other[:, hd:]], 1)
    d_part = nt(g_all, w_all).astype(bf16)
    d_tokens = ring_reduce(
        d_part.reshape(4, tok_rows // 8, -1), y, lambda b, d: head_move(b, dy=d)
    ).astype(bf16)

    def finish(total):
        mine = lax.dynamic_slice_in_dim(total, core * own_rows, own_rows, 0)
        send = lax.dynamic_slice_in_dim(total, (1 - core) * own_rows, own_rows, 0)
        return pair_cols(even, mine, swap_cores(send))

    kq0, kq1 = finish(wq_z)
    kk, kv_ = finish(wkv_z)
    summed = jnp.concatenate([kq0, kq1, kk, kv_], 1)
    gradient = (summed / scale_power).reshape(own_rows, 1, 4 * hd)
    first_new = beta_one * adam_first + (1.0 - beta_one) * gradient
    second_new = beta_two * adam_second + (1.0 - beta_two) * gradient * gradient
    first_fix = 1.0 - beta_one**ADAM_STEP
    second_fix = 1.0 - beta_two**ADAM_STEP
    update = first_new / first_fix / (jnp.sqrt(second_new / second_fix) + adam_eps)
    master_new = qkv_master - learn_rate * (update + weight_decay * qkv_master)
    applied = (lax.dynamic_slice_in_dim(skip_flag, head_pos, 1, 0) == 0)[None, :, None]
    return (
        attn_out,
        d_tokens,
        jnp.where(applied, master_new, qkv_master),
        jnp.where(applied, first_new, adam_first),
        jnp.where(applied, second_new, adam_second),
    )


def solution(mesh):
    return jax.shard_map(
        per_device,
        mesh=mesh,
        in_specs=(
            P("seq", None),
            P("seq", "head"),
            P("seq", "head", None),
            P("seq", "head", None),
            P("seq", "head", None),
            P(),
            P(),
        ),
        out_specs=(
            P("seq", "head"),
            P(("seq", "head"), None),
            P("seq", "head", None),
            P("seq", "head", None),
            P("seq", "head", None),
        ),
        check_vma=False,
    )
```

```python
import jax
import jax.numpy as jnp
from jax import lax
from jax.experimental import pallas as pl
from jax.experimental.pallas import tpu as pltpu
from jax.sharding import PartitionSpec as P

HEAD_DIM = 128
ATTEND_SPAN = 1024
ATTN_SCALAR = 168
Q_PER_KV = 2
ADAM_STEP = 1000

norm_eps = 1e-06
beta_one = 0.9
beta_two = 0.95
adam_eps = 1e-08
learn_rate = 0.01
weight_decay = 0.1

bf16 = jnp.bfloat16
f32 = jnp.float32

SEQ = 32
HEAD = 8


def seq_move(block, dx=0, dz=0, swap=False):
    pairs = []
    for s in range(SEQ):
        x, z, c = s // 8, (s // 2) % 4, s % 2
        pairs.append((s, ((x + dx) % 4) * 8 + ((z + dz) % 4) * 2 + (c ^ int(swap))))
    return lax.ppermute(block, "seq", pairs)


def head_move(block, dy=0, flip=False):
    pairs = []
    for h in range(HEAD):
        half, y = h // 4, h % 4
        pairs.append((h, (half ^ int(flip)) * 4 + (y + dy) % 4))
    return lax.ppermute(block, "head", pairs)


def swap_cores(block):
    return seq_move(block, swap=True)


def shifted(block, distance):
    route = [(i - distance, i) for i in range(SEQ) if 0 <= i - distance < SEQ]
    return lax.ppermute(block, "seq", route)


def tie(later, *earlier):
    return lax.optimization_barrier((later,) + earlier)[0]


def place(blocks, spots):
    out = jnp.broadcast_to(blocks[0][None], (4,) + blocks[0].shape)
    for block, spot in zip(blocks[1:], spots[1:]):
        out = lax.dynamic_update_slice(out, block[None], (spot,) + (0,) * block.ndim)
    return out.reshape((-1,) + blocks[0].shape[1:])


def gather_z(block, z):
    parts = [block] + [seq_move(block, dz=k) for k in (1, 2, 3)]
    return place(parts, [(z - k) % 4 for k in range(4)])


def gather_x(block, x, after=None, events=None):
    half = block.shape[0] // 2
    left = seq_move(block, dx=1)
    right = seq_move(block, dx=-1)
    if events is not None:
        events.append((left, right))
    if after is not None:
        left, right, _ = lax.optimization_barrier((left, right, after))
    far_top = seq_move(left[:half], dx=1)
    far_low = seq_move(right[half:], dx=-1)
    far = jnp.concatenate([far_top, far_low], 0)
    return place([block, left, far, right], [x, (x - 1) % 4, (x + 2) % 4, (x + 1) % 4])


def ring_reduce(blocks, pos, move, events=None):
    half = blocks.shape[1] // 2
    pick = lambda k: lax.dynamic_index_in_dim(blocks, (pos + k) % 4, 0, keepdims=False)
    own, ahead, far, back = pick(0), pick(1), pick(2), pick(3)
    top = move(far[:half], 1)
    low = move(far[half:], -1)
    if events is not None:
        events.append((top, low))
    ahead = jnp.concatenate(
        [(ahead[:half].astype(f32) + top.astype(f32)).astype(bf16), ahead[half:]], 0
    )
    back = jnp.concatenate(
        [back[:half], (back[half:].astype(f32) + low.astype(f32)).astype(bf16)], 0
    )
    from_back = move(ahead, 1)
    from_ahead = move(back, -1)
    return own.astype(f32) + from_back.astype(f32) + from_ahead.astype(f32)


def reduce_x(total, x, events=None):
    blocks = total.reshape(4, -1, total.shape[1])
    return ring_reduce(blocks, x, lambda b, d: seq_move(b, dx=d), events)


def reduce_z(total, z):
    blocks = total.reshape(4, -1, total.shape[1])
    pick = lambda k: lax.dynamic_index_in_dim(blocks, (z + k) % 4, 0, keepdims=False)
    out = pick(0).astype(f32)
    for k in (1, 2, 3):
        out = out + seq_move(pick(k), dz=k).astype(f32)
    return out


def head_norm(raw_vals):
    factor = lax.rsqrt(jnp.mean(raw_vals * raw_vals, axis=-1, keepdims=True) + norm_eps)
    return (raw_vals * factor, factor)


def norm_back(raw_vals, factor, grad_in):
    inner_mean = jnp.mean(raw_vals * grad_in, axis=-1, keepdims=True)
    return factor * grad_in - raw_vals * factor * factor * factor * inner_mean


def window_kernel(query_tile, key_tile, query_start, key_start):
    score_scale = float(ATTN_SCALAR) ** (-0.5)
    scores = (
        jnp.einsum("tqd,ld->qtl", query_tile, key_tile, preferred_element_type=f32) * score_scale
    )
    query_pos = query_start + jnp.arange(query_tile.shape[0], dtype=jnp.int32)
    key_pos = key_start + jnp.arange(key_tile.shape[0], dtype=jnp.int32)
    gap_len = query_pos[:, None] - key_pos[None, :]
    allowed = (key_pos[None, :] >= 0) & (gap_len >= 0) & (gap_len < ATTEND_SPAN)
    return jnp.where(allowed, jnp.exp(scores), 0.0)


def pair_cols(even, a, b):
    return jnp.where(even, a, b), jnp.where(even, b, a)


def rows_pair(even, mine, theirs):
    return jnp.where(even, jnp.concatenate([mine, theirs], 0), jnp.concatenate([theirs, mine], 0))


def nt(a, b):
    return lax.dot_general(a, b, (((1,), (1,)), ((), ())), preferred_element_type=f32)


def tn(a, b):
    return lax.dot_general(a, b, (((0,), (0,)), ((), ())), preferred_element_type=f32)


TILE = 896


def term_kernel(n_ref, g_ref, keep_ref, send_ref):
    out = tn(n_ref[...], g_ref[...])
    keep_ref[...] = out[:, :HEAD_DIM].astype(bf16)
    send_ref[...] = out[:, HEAD_DIM:].astype(bf16)


def weight_terms(normed, pair):
    rows, width = normed.shape
    shape = jax.ShapeDtypeStruct((width, HEAD_DIM), bf16)
    return pl.pallas_call(
        term_kernel,
        grid=(width // TILE,),
        in_specs=[
            pl.BlockSpec((rows, TILE), lambda i: (0, i)),
            pl.BlockSpec((rows, 2 * HEAD_DIM), lambda i: (0, 0)),
        ],
        out_specs=[pl.BlockSpec((TILE, HEAD_DIM), lambda i: (i, 0))] * 2,
        out_shape=[shape, shape],
        name="weight_terms",
    )(normed, pair)


def tokens_kernel(a_ref, b_ref, c_ref, d_ref, ka_ref, kb_ref, qa_ref, qb_ref, fa_ref, fb_ref, o_ref):
    hd = HEAD_DIM
    acc = nt(a_ref[...], jnp.concatenate([ka_ref[...], kb_ref[...]], 1))
    acc += nt(b_ref[...], jnp.concatenate([qa_ref[...], qb_ref[...]], 1))
    acc += nt(c_ref[...], jnp.concatenate([fa_ref[:, :hd], fb_ref[:, :hd]], 1))
    acc += nt(d_ref[...], jnp.concatenate([fa_ref[:, hd:], fb_ref[:, hd:]], 1))
    o_ref[...] = acc.astype(bf16)


def token_terms(grads, narrow, wide):
    rows = grads[0].shape[0]
    width = wide[0].shape[0]
    hd = HEAD_DIM
    return pl.pallas_call(
        tokens_kernel,
        grid=(width // TILE,),
        in_specs=[pl.BlockSpec((rows, 2 * hd), lambda i: (0, 0))] * 4
        + [pl.BlockSpec((TILE, hd), lambda i: (i, 0))] * 4
        + [pl.BlockSpec((TILE, 2 * hd), lambda i: (i, 0))] * 2,
        out_specs=pl.BlockSpec((rows, TILE), lambda i: (0, i)),
        out_shape=jax.ShapeDtypeStruct((rows, width), bf16),
        name="token_terms",
    )(*grads, *narrow, *wide)


def per_device(normed, cotangent, qkv_master, adam_first, adam_second, skip_flag, scale_exponent):
    tok_rows = normed.shape[0]
    hd = HEAD_DIM
    own_rows = qkv_master.shape[0]
    halo_span = ATTEND_SPAN // tok_rows
    score_scale = float(ATTN_SCALAR) ** (-0.5)
    seq_pos = lax.axis_index("seq")
    head_pos = lax.axis_index("head")
    x, z, core = seq_pos // 8, (seq_pos // 2) % 4, seq_pos % 2
    y, half = head_pos % 4, head_pos // 4
    even = core == 0

    master16 = qkv_master.reshape(own_rows, 4 * hd).astype(bf16)
    cols = [master16[:, i * hd : (i + 1) * hd] for i in range(4)]
    kv_mine, kv_theirs = pair_cols(even, cols[2], cols[3])
    q_mine, q_theirs = pair_cols(even, cols[0], cols[1])
    got = swap_cores(jnp.concatenate([kv_theirs, q_theirs], 1))
    kv_block = rows_pair(even, kv_mine, got[:, :hd])
    q_block = rows_pair(even, q_mine, got[:, hd:])
    kv_plane = gather_z(kv_block, z)
    q_plane = gather_z(q_block, z)
    far_block = head_move(
        tie(jnp.concatenate([kv_block, q_block], 1), q_plane), flip=True
    )
    kv_first = []
    kv_weights = gather_x(kv_plane, x, events=kv_first)
    kv_other = swap_cores(kv_weights)
    q_weights = gather_x(q_plane, x)
    q_other = swap_cores(q_weights)
    w_kv = jnp.concatenate([kv_weights, kv_other], 1)
    w_q = jnp.concatenate([q_weights, q_other], 1)
    far_plane = gather_z(tie(far_block, *kv_first[0]), z)

    kv = jnp.dot(normed, w_kv, preferred_element_type=f32)
    k_raw, v_raw = pair_cols(even, kv[:, :hd], kv[:, hd:])
    k_unit, k_factor = head_norm(k_raw)
    kv16 = jnp.concatenate([k_unit.astype(bf16), v_raw.astype(bf16)], 1)
    far_plane = tie(far_plane, kv16)
    ext = jnp.concatenate([shifted(kv16, 2), shifted(kv16, 1), kv16], 0)
    ext_keys, ext_values = ext[:, :hd], ext[:, hd:]

    qm = jnp.dot(normed, w_q, preferred_element_type=f32)
    q_a, q_b = pair_cols(even, qm[:, :hd], qm[:, hd:])
    q_raw = jnp.stack([q_a, q_b], 1)
    q_unit, q_factor = head_norm(q_raw)
    queries = q_unit.astype(bf16)

    query_start = seq_pos * tok_rows
    key_start = query_start - halo_span * tok_rows
    kernel = window_kernel(queries, ext_keys, query_start, key_start)
    totals = jnp.sum(kernel, axis=-1, keepdims=True)
    prob_tile = (kernel / totals).astype(bf16)
    far_weights = gather_x(far_plane, x, after=prob_tile)
    mixed = jnp.einsum("qtl,ld->tqd", prob_tile, ext_values, preferred_element_type=f32)
    attn_out = mixed.astype(bf16).reshape(tok_rows, Q_PER_KV * hd)
    scale_power = jnp.left_shift(jnp.int32(1), scale_exponent[0]).astype(f32)
    grad_out = (cotangent.astype(f32) * scale_power).astype(bf16)
    grad_out = grad_out.reshape(tok_rows, Q_PER_KV, hd)
    row_delta = jnp.transpose(jnp.sum(grad_out.astype(f32) * mixed, axis=-1), (1, 0))
    grad_probs = jnp.einsum("tqd,ld->qtl", grad_out, ext_values, preferred_element_type=f32)
    grad_scores = (
        prob_tile.astype(f32) * (grad_probs - row_delta[..., None]) * score_scale
    ).astype(bf16)
    grad_keys_ext = jnp.einsum("qtl,tqd->ld", grad_scores, queries, preferred_element_type=f32)
    grad_values_ext = jnp.einsum("qtl,tqd->ld", prob_tile, grad_out, preferred_element_type=f32)
    grad_kv = [
        jnp.concatenate(
            [grad_keys_ext[i * tok_rows : (i + 1) * tok_rows],
             grad_values_ext[i * tok_rows : (i + 1) * tok_rows]], 1)
        for i in range(3)
    ]
    back_one = shifted(grad_kv[1].astype(bf16), -1)
    back_two = shifted(grad_kv[0].astype(bf16), -2)
    grad_queries = jnp.einsum("qtl,ld->tqd", grad_scores, ext_keys, preferred_element_type=f32)

    g_q = norm_back(q_raw, q_factor, grad_queries).astype(bf16)
    gq_mine, gq_theirs = pair_cols(even, g_q[:, 0], g_q[:, 1])

    def exchange_half(g):
        own_half = lax.dynamic_slice_in_dim(g, half * (tok_rows // 2), tok_rows // 2, 0)
        far_half = lax.dynamic_slice_in_dim(g, (1 - half) * (tok_rows // 2), tok_rows // 2, 0)
        return own_half, head_move(far_half, flip=True)

    def weight_sum(pair):
        keep, send = weight_terms(normed, pair)
        return (keep.astype(f32) + swap_cores(send).astype(f32)).astype(bf16)

    gq_pair = jnp.concatenate([gq_mine, gq_theirs], 1)
    gq_own, gq_far = exchange_half(gq_pair)
    q_first = []
    wq_x = reduce_x(weight_sum(gq_pair), x, q_first).astype(bf16)
    far_other = swap_cores(tie(far_weights, g_q))

    grad_kv_sum = grad_kv[2] + back_one.astype(f32) + back_two.astype(f32)
    g_k = norm_back(k_raw, k_factor, grad_kv_sum[:, :hd]).astype(bf16)
    g_v = grad_kv_sum[:, hd:].astype(bf16)
    gkv_mine, gkv_theirs = pair_cols(even, g_k, g_v)
    gkv_pair = jnp.concatenate([gkv_mine, gkv_theirs], 1)
    gkv_own, gkv_far = exchange_half(gkv_pair)
    wkv_sum = weight_sum(gkv_pair)

    d_part = token_terms(
        (tie(gkv_own, *q_first[0]), gq_own, gkv_far, gq_far),
        (kv_weights, kv_other, q_weights, q_other),
        (far_weights, far_other),
    )
    wq_z = reduce_z(tie(wq_x, d_part), z)
    wkv_x = reduce_x(tie(wkv_sum, d_part), x).astype(bf16)
    wkv_z = reduce_z(wkv_x, z)
    d_tokens = ring_reduce(
        d_part.reshape(4, tok_rows // 8, -1), y, lambda b, d: head_move(b, dy=d)
    ).astype(bf16)

    def finish(total):
        mine = lax.dynamic_slice_in_dim(total, core * own_rows, own_rows, 0)
        send = lax.dynamic_slice_in_dim(total, (1 - core) * own_rows, own_rows, 0)
        return pair_cols(even, mine, swap_cores(send))

    kq0, kq1 = finish(wq_z)
    kk, kv_ = finish(wkv_z)
    summed = jnp.concatenate([kq0, kq1, kk, kv_], 1)
    gradient = (summed / scale_power).reshape(own_rows, 1, 4 * hd)
    first_new = beta_one * adam_first + (1.0 - beta_one) * gradient
    second_new = beta_two * adam_second + (1.0 - beta_two) * gradient * gradient
    first_fix = 1.0 - beta_one**ADAM_STEP
    second_fix = 1.0 - beta_two**ADAM_STEP
    update = first_new / first_fix / (jnp.sqrt(second_new / second_fix) + adam_eps)
    master_new = qkv_master - learn_rate * (update + weight_decay * qkv_master)
    applied = (lax.dynamic_slice_in_dim(skip_flag, head_pos, 1, 0) == 0)[None, :, None]
    return (
        attn_out,
        d_tokens,
        jnp.where(applied, master_new, qkv_master),
        jnp.where(applied, first_new, adam_first),
        jnp.where(applied, second_new, adam_second),
    )


def solution(mesh):
    return jax.shard_map(
        per_device,
        mesh=mesh,
        in_specs=(
            P("seq", None),
            P("seq", "head"),
            P("seq", "head", None),
            P("seq", "head", None),
            P("seq", "head", None),
            P(),
            P(),
        ),
        out_specs=(
            P("seq", "head"),
            P(("seq", "head"), None),
            P("seq", "head", None),
            P("seq", "head", None),
            P("seq", "head", None),
        ),
        check_vma=False,
    )
```

```python
import jax
import jax.numpy as jnp
from jax import lax
from jax.experimental import pallas as pl
from jax.experimental.pallas import tpu as pltpu
from jax.sharding import PartitionSpec as P

HEAD_DIM = 128
ATTEND_SPAN = 1024
ATTN_SCALAR = 168
Q_PER_KV = 2
ADAM_STEP = 1000

norm_eps = 1e-06
beta_one = 0.9
beta_two = 0.95
adam_eps = 1e-08
learn_rate = 0.01
weight_decay = 0.1

bf16 = jnp.bfloat16
f32 = jnp.float32

SEQ = 32
HEAD = 8


def seq_move(block, dx=0, dz=0, swap=False):
    pairs = []
    for s in range(SEQ):
        x, z, c = s // 8, (s // 2) % 4, s % 2
        pairs.append((s, ((x + dx) % 4) * 8 + ((z + dz) % 4) * 2 + (c ^ int(swap))))
    return lax.ppermute(block, "seq", pairs)


def head_move(block, dy=0, flip=False):
    pairs = []
    for h in range(HEAD):
        half, y = h // 4, h % 4
        pairs.append((h, (half ^ int(flip)) * 4 + (y + dy) % 4))
    return lax.ppermute(block, "head", pairs)


def swap_cores(block):
    return seq_move(block, swap=True)


def shifted(block, distance):
    route = [(i - distance, i) for i in range(SEQ) if 0 <= i - distance < SEQ]
    return lax.ppermute(block, "seq", route)


def tie(later, *earlier):
    return lax.optimization_barrier((later,) + earlier)[0]


def place(blocks, spots):
    out = jnp.broadcast_to(blocks[0][None], (4,) + blocks[0].shape)
    for block, spot in zip(blocks[1:], spots[1:]):
        out = lax.dynamic_update_slice(out, block[None], (spot,) + (0,) * block.ndim)
    return out.reshape((-1,) + blocks[0].shape[1:])


def gather_z(block, z):
    parts = [block] + [seq_move(block, dz=k) for k in (1, 2, 3)]
    return place(parts, [(z - k) % 4 for k in range(4)])


def spread_x(block):
    return [seq_move(block, dx=k) for k in (1, 3, 2)]


def join_x(block, parts, x):
    return place([block] + parts, [x, (x - 1) % 4, (x + 1) % 4, (x + 2) % 4])


def send_parts(total, pos, move):
    blocks = total.reshape(4, -1, total.shape[1])
    pick = lambda k: lax.dynamic_index_in_dim(blocks, (pos + k) % 4, 0, keepdims=False)
    return [pick(0)] + [move(pick(k), k) for k in (1, 3, 2)]


def add_parts(parts):
    return sum(p.astype(f32) for p in parts[1:]) + parts[0].astype(f32)


def head_norm(raw_vals):
    factor = lax.rsqrt(jnp.mean(raw_vals * raw_vals, axis=-1, keepdims=True) + norm_eps)
    return (raw_vals * factor, factor)


def norm_back(raw_vals, factor, grad_in):
    inner_mean = jnp.mean(raw_vals * grad_in, axis=-1, keepdims=True)
    return factor * grad_in - raw_vals * factor * factor * factor * inner_mean


def pair_cols(even, a, b):
    return jnp.where(even, a, b), jnp.where(even, b, a)


def rows_pair(even, mine, theirs):
    return jnp.where(even, jnp.concatenate([mine, theirs], 0), jnp.concatenate([theirs, mine], 0))


def nt(a, b):
    return lax.dot_general(a, b, (((1,), (1,)), ((), ())), preferred_element_type=f32)


def tn(a, b):
    return lax.dot_general(a, b, (((0,), (0,)), ((), ())), preferred_element_type=f32)


TILE = 896


def term_kernel(n_ref, g_ref, keep_ref, send_ref, turned):
    @pl.when(pl.program_id(0) == 0)
    def _():
        turned[...] = g_ref[...].T

    out = jnp.dot(turned[...], n_ref[...], preferred_element_type=f32).astype(bf16).T
    keep_ref[...] = out[:, :HEAD_DIM]
    send_ref[...] = out[:, HEAD_DIM:]


def weight_terms(normed, pair):
    rows, width = normed.shape
    shape = jax.ShapeDtypeStruct((width, HEAD_DIM), bf16)
    return pl.pallas_call(
        term_kernel,
        grid=(width // TILE,),
        in_specs=[
            pl.BlockSpec((rows, TILE), lambda i: (0, i)),
            pl.BlockSpec((rows, 2 * HEAD_DIM), lambda i: (0, 0)),
        ],
        out_specs=[pl.BlockSpec((TILE, HEAD_DIM), lambda i: (i, 0))] * 2,
        out_shape=[shape, shape],
        scratch_shapes=[pltpu.VMEM((2 * HEAD_DIM, rows), bf16)],
        name="weight_terms",
    )(normed, pair)


def tokens_kernel(own_ref, far_ref, ka_ref, kb_ref, qa_ref, qb_ref, fa_ref, fb_ref, o_ref, turned):
    hd = HEAD_DIM

    @pl.when(pl.program_id(0) == 0)
    def _():
        turned[: 4 * hd] = own_ref[...].T
        turned[4 * hd :] = far_ref[...].T

    rows = jnp.concatenate(
        [ka_ref[...], kb_ref[...], qa_ref[...], qb_ref[...],
         fa_ref[:, :hd], fb_ref[:, :hd], fa_ref[:, hd:], fb_ref[:, hd:]], 1)
    acc = jnp.dot(rows, turned[...], preferred_element_type=f32)
    o_ref[...] = acc.astype(bf16).T


def token_terms(own, far, narrow, wide):
    rows, cols = own.shape
    width = wide[0].shape[0]
    hd = HEAD_DIM
    return pl.pallas_call(
        tokens_kernel,
        grid=(width // TILE,),
        in_specs=[pl.BlockSpec((rows, cols), lambda i: (0, 0))] * 2
        + [pl.BlockSpec((TILE, hd), lambda i: (i, 0))] * 4
        + [pl.BlockSpec((TILE, 2 * hd), lambda i: (i, 0))] * 2,
        out_specs=pl.BlockSpec((rows, TILE), lambda i: (0, i)),
        out_shape=jax.ShapeDtypeStruct((rows, width), bf16),
        scratch_shapes=[pltpu.VMEM((2 * cols, rows), bf16)],
        name="token_terms",
    )(own, far, *narrow, *wide)


Q_TILE = 256


def attend_kernel(pos_ref, power_ref, q_ref, two_ref, one_ref, own_ref, cot_ref,
                  out_ref, gq_ref, two_out, one_out, own_out, ext, acc):
    hd = HEAD_DIM
    rows = own_ref.shape[0]
    step = pl.program_id(0)
    start = pl.multiple_of((step // 2) * Q_TILE, Q_TILE)
    span = ATTEND_SPAN + Q_TILE
    scale = float(ATTN_SCALAR) ** (-0.5)

    @pl.when(step == 0)
    def _():
        ext[:rows] = two_ref[...]
        ext[rows : 2 * rows] = one_ref[...]
        ext[2 * rows :] = own_ref[...]
        acc[...] = jnp.zeros_like(acc)

    q_raw = q_ref[...]
    factor = lax.rsqrt(jnp.mean(q_raw * q_raw, axis=1, keepdims=True) + norm_eps)
    queries = (q_raw * factor).astype(bf16)
    keys = ext[pl.ds(start, span), :hd]
    values = ext[pl.ds(start, span), hd:]
    scores = nt(queries, keys) * scale
    spot = lax.broadcasted_iota(jnp.int32, scores.shape, 1)
    gap = lax.broadcasted_iota(jnp.int32, scores.shape, 0) + ATTEND_SPAN - spot
    first = ATTEND_SPAN - pos_ref[0] * rows - start
    allowed = (gap >= 0) & (gap < ATTEND_SPAN) & (spot >= first)
    kernel = jnp.where(allowed, jnp.exp(scores), 0.0)
    totals = jnp.sum(kernel, axis=1, keepdims=True)
    probs = (kernel / totals).astype(bf16)
    mixed = jnp.dot(probs, values, preferred_element_type=f32)
    out_ref[...] = mixed.astype(bf16)
    grad_out = (cot_ref[...].astype(f32) * power_ref[0]).astype(bf16)
    delta = jnp.sum(grad_out.astype(f32) * mixed, axis=1, keepdims=True)
    grad_probs = nt(grad_out, values)
    grad_scores = (probs.astype(f32) * (grad_probs - delta) * scale).astype(bf16)
    grad_q = jnp.dot(grad_scores, keys, preferred_element_type=f32)
    inner = jnp.mean(q_raw * grad_q, axis=1, keepdims=True)
    gq_ref[...] = (factor * grad_q - q_raw * factor * factor * factor * inner).astype(bf16)
    acc[pl.ds(start, span), :hd] += tn(grad_scores, queries)
    acc[pl.ds(start, span), hd:] += tn(probs, grad_out)

    @pl.when(step == pl.num_programs(0) - 1)
    def _():
        two_out[...] = acc[:rows].astype(bf16)
        one_out[...] = acc[rows : 2 * rows].astype(bf16)
        own_out[...] = acc[2 * rows :]


def attend(pos, power, q_cols, two, one, own, cotangent):
    rows = own.shape[0]
    hd = HEAD_DIM
    whole = pl.BlockSpec((rows, 2 * hd), lambda i, p: (0, 0))
    plain = pl.BlockSpec((Q_TILE, hd), lambda i, p: (i // 2, i % 2))
    turned = pl.BlockSpec((Q_TILE, hd), lambda i, p: (i // 2, (i + p[1]) % 2))
    shape = lambda kind: jax.ShapeDtypeStruct((rows, 2 * hd), kind)
    return pl.pallas_call(
        attend_kernel,
        grid_spec=pltpu.PrefetchScalarGridSpec(
            num_scalar_prefetch=1,
            grid=(2 * rows // Q_TILE,),
            in_specs=[pl.BlockSpec(memory_space=pltpu.SMEM), turned, whole, whole, whole, plain],
            out_specs=[plain, turned, whole, whole, whole],
            scratch_shapes=[
                pltpu.VMEM((ATTEND_SPAN + rows, 2 * hd), bf16),
                pltpu.VMEM((ATTEND_SPAN + rows, 2 * hd), f32),
            ],
        ),
        out_shape=[shape(bf16), shape(bf16), shape(bf16), shape(bf16), shape(f32)],
        name="attend",
    )(pos, power, q_cols, two, one, own, cotangent)


def step_kernel(info_ref, power_ref, mine_ref, got_ref, master_ref, first_ref, second_ref,
                master_out, first_out, second_out):
    hd = HEAD_DIM
    even = info_ref[0] == 0
    mine, got = mine_ref[...], got_ref[...]
    lead = jnp.where(even, mine, got)
    trail = jnp.where(even, got, mine)
    summed = jnp.concatenate([lead[:, hd:], trail[:, hd:], lead[:, :hd], trail[:, :hd]], 1)
    gradient = summed / power_ref[0]
    master, first, second = master_ref[...], first_ref[...], second_ref[...]
    first_new = beta_one * first + (1.0 - beta_one) * gradient
    second_new = beta_two * second + (1.0 - beta_two) * gradient * gradient
    first_fix = 1.0 - beta_one**ADAM_STEP
    second_fix = 1.0 - beta_two**ADAM_STEP
    update = first_new / first_fix / (jnp.sqrt(second_new / second_fix) + adam_eps)
    applied = info_ref[1] == 0
    master_out[...] = jnp.where(
        applied, master - learn_rate * (update + weight_decay * master), master
    )
    first_out[...] = jnp.where(applied, first_new, first)
    second_out[...] = jnp.where(applied, second_new, second)


def adam_step(info, power, mine, got, master, first, second):
    rows, cols = master.shape
    tile = 56
    half = pl.BlockSpec((tile, cols // 2), lambda i, p: (i, 0))
    full = pl.BlockSpec((tile, cols), lambda i, p: (i, 0))
    return pl.pallas_call(
        step_kernel,
        grid_spec=pltpu.PrefetchScalarGridSpec(
            num_scalar_prefetch=1,
            grid=(rows // tile,),
            in_specs=[pl.BlockSpec(memory_space=pltpu.SMEM), half, half, full, full, full],
            out_specs=[full, full, full],
        ),
        out_shape=[jax.ShapeDtypeStruct((rows, cols), f32)] * 3,
        name="adam_step",
    )(info, power, mine, got, master, first, second)


def per_device(normed, cotangent, qkv_master, adam_first, adam_second, skip_flag, scale_exponent):
    tok_rows = normed.shape[0]
    hd = HEAD_DIM
    own_rows = qkv_master.shape[0]
    seq_pos = lax.axis_index("seq")
    head_pos = lax.axis_index("head")
    x, z, core = seq_pos // 8, (seq_pos // 2) % 4, seq_pos % 2
    half = head_pos // 4
    even = core == 0

    master16 = qkv_master.reshape(own_rows, 4 * hd).astype(bf16)
    cols = [master16[:, i * hd : (i + 1) * hd] for i in range(4)]
    kv_mine, kv_theirs = pair_cols(even, cols[2], cols[3])
    q_mine, q_theirs = pair_cols(even, cols[0], cols[1])
    got = swap_cores(jnp.concatenate([kv_theirs, q_theirs], 1))
    kv_block = rows_pair(even, kv_mine, got[:, :hd])
    q_block = rows_pair(even, q_mine, got[:, hd:])
    plane = gather_z(jnp.concatenate([kv_block, q_block], 1), z)
    far_block = head_move(tie(jnp.concatenate([kv_block, q_block], 1), plane), flip=True)
    kv_plane, q_plane = plane[:, :hd], plane[:, hd:]
    kv_parts = spread_x(kv_plane)
    q_parts = spread_x(tie(q_plane, kv_plane))
    far_plane = gather_z(tie(far_block, *kv_parts), z)
    kv_weights = join_x(kv_plane, kv_parts, x)
    kv_other = swap_cores(kv_weights)
    q_weights = join_x(q_plane, q_parts, x)
    q_other = swap_cores(q_weights)

    kv = jnp.dot(normed, jnp.concatenate([kv_weights, kv_other], 1), preferred_element_type=f32)
    k_raw, v_raw = pair_cols(even, kv[:, :hd], kv[:, hd:])
    k_unit, k_factor = head_norm(k_raw)
    kv16 = jnp.concatenate([k_unit.astype(bf16), v_raw.astype(bf16)], 1)
    kv_two, kv_one = shifted(kv16, 2), shifted(kv16, 1)
    far_plane = tie(far_plane, kv16)
    far_parts = spread_x(far_plane)

    q_cols = jnp.dot(normed, jnp.concatenate([q_weights, q_other], 1), preferred_element_type=f32)
    scale_power = jnp.left_shift(jnp.int32(1), scale_exponent).astype(f32)
    attn_out, gq_pair, part_two, part_one, part_own = attend(
        jnp.stack([seq_pos, core]), scale_power, q_cols, kv_two, kv_one, kv16, cotangent
    )
    back_two, back_one = shifted(part_two, -2), shifted(part_one, -1)

    def weight_sum(pair):
        keep, send = weight_terms(normed, pair)
        return (keep.astype(f32) + swap_cores(send).astype(f32)).astype(bf16)

    move_x = lambda b, k: seq_move(b, dx=k)
    wq_parts = send_parts(weight_sum(gq_pair), x, move_x)
    far_tied = lax.optimization_barrier((gq_pair, *far_parts))[1:]
    far_weights = join_x(far_plane, list(far_tied), x)
    far_other = swap_cores(far_weights)

    grad_kv = part_own + back_one.astype(f32) + back_two.astype(f32)
    g_k = norm_back(k_raw, k_factor, grad_kv[:, :hd]).astype(bf16)
    g_v = grad_kv[:, hd:].astype(bf16)
    gkv_pair = jnp.concatenate(pair_cols(even, g_k, g_v), 1)
    wkv_parts = send_parts(weight_sum(gkv_pair), x, move_x)

    g_all = jnp.concatenate([gkv_pair, gq_pair], 1)
    own_half = lax.dynamic_slice_in_dim(g_all, half * (tok_rows // 2), tok_rows // 2, 0)
    far_half = lax.dynamic_slice_in_dim(g_all, (1 - half) * (tok_rows // 2), tok_rows // 2, 0)
    d_part = token_terms(
        own_half,
        head_move(far_half, flip=True),
        (kv_weights, kv_other, q_weights, q_other),
        (far_weights, far_other),
    )
    d_blocks = lax.all_to_all(
        d_part.reshape(4, tok_rows // 8, -1), "head", split_axis=0, concat_axis=0, tiled=True,
        axis_index_groups=[[0, 1, 2, 3], [4, 5, 6, 7]],
    )
    d_tokens = add_parts([d_blocks[k] for k in range(4)]).astype(bf16)

    tied = lax.optimization_barrier((d_part, *wq_parts, *wkv_parts))[1:]
    w_x = jnp.concatenate(
        [add_parts(tied[4:]).astype(bf16), add_parts(tied[:4]).astype(bf16)], 1
    )
    w_z = add_parts(send_parts(w_x, z, lambda b, k: seq_move(b, dz=k)))

    mine = lax.dynamic_slice_in_dim(w_z, core * own_rows, own_rows, 0)
    got = swap_cores(lax.dynamic_slice_in_dim(w_z, (1 - core) * own_rows, own_rows, 0))
    flag = lax.dynamic_index_in_dim(skip_flag, head_pos, 0, keepdims=False)
    flat = lambda a: a.reshape(own_rows, 4 * hd)
    new = adam_step(
        jnp.stack([core, flag]), scale_power, mine, got,
        flat(qkv_master), flat(adam_first), flat(adam_second),
    )
    return (attn_out, d_tokens) + tuple(a.reshape(qkv_master.shape) for a in new)


def solution(mesh):
    return jax.shard_map(
        per_device,
        mesh=mesh,
        in_specs=(
            P("seq", None),
            P("seq", "head"),
            P("seq", "head", None),
            P("seq", "head", None),
            P("seq", "head", None),
            P(),
            P(),
        ),
        out_specs=(
            P("seq", "head"),
            P(("seq", "head"), None),
            P("seq", "head", None),
            P("seq", "head", None),
            P("seq", "head", None),
        ),
        check_vma=False,
    )
```

```python
import jax
import jax.numpy as jnp
from jax import lax
from jax.experimental import pallas as pl
from jax.experimental.pallas import tpu as pltpu
from jax.sharding import PartitionSpec as P

HEAD_DIM = 128
ATTEND_SPAN = 1024
ATTN_SCALAR = 168
ADAM_STEP = 1000

norm_eps = 1e-06
beta_one = 0.9
beta_two = 0.95
adam_eps = 1e-08
learn_rate = 0.01
weight_decay = 0.1

bf16 = jnp.bfloat16
f32 = jnp.float32

SEQ = 32
HEAD = 8


def seq_move(block, dx=0, dz=0, swap=False):
    pairs = []
    for s in range(SEQ):
        x, z, c = s // 8, (s // 2) % 4, s % 2
        pairs.append((s, ((x + dx) % 4) * 8 + ((z + dz) % 4) * 2 + (c ^ int(swap))))
    return lax.ppermute(block, "seq", pairs)


def head_move(block, dy=0, flip=False):
    pairs = []
    for h in range(HEAD):
        half, y = h // 4, h % 4
        pairs.append((h, (half ^ int(flip)) * 4 + (y + dy) % 4))
    return lax.ppermute(block, "head", pairs)


def swap_cores(block):
    return seq_move(block, swap=True)


def shifted(block, distance):
    route = [(i - distance, i) for i in range(SEQ) if 0 <= i - distance < SEQ]
    return lax.ppermute(block, "seq", route)


def tie(later, *earlier):
    return lax.optimization_barrier((later,) + earlier)[0]


def place(blocks, spots):
    out = jnp.broadcast_to(blocks[0][None], (4,) + blocks[0].shape)
    for block, spot in zip(blocks[1:], spots[1:]):
        out = lax.dynamic_update_slice(out, block[None], (spot,) + (0,) * block.ndim)
    return out.reshape((-1,) + blocks[0].shape[1:])


def gather_z(block, z):
    parts = [block] + [seq_move(block, dz=k) for k in (1, 2, 3)]
    return place(parts, [(z - k) % 4 for k in range(4)])


def spread_x(block):
    return [seq_move(block, dx=k) for k in (1, 3, 2)]


def join_x(block, parts, x):
    return place([block] + parts, [x, (x - 1) % 4, (x + 1) % 4, (x + 2) % 4])


def send_parts(total, pos, move):
    blocks = total.reshape(4, -1, total.shape[1])
    pick = lambda k: lax.dynamic_index_in_dim(blocks, (pos + k) % 4, 0, keepdims=False)
    return [pick(0)] + [move(pick(k), k) for k in (1, 3, 2)]


def add_parts(parts):
    return sum(p.astype(f32) for p in parts[1:]) + parts[0].astype(f32)


def head_norm(raw_vals):
    factor = lax.rsqrt(jnp.mean(raw_vals * raw_vals, axis=-1, keepdims=True) + norm_eps)
    return (raw_vals * factor, factor)


def norm_back(raw_vals, factor, grad_in):
    inner_mean = jnp.mean(raw_vals * grad_in, axis=-1, keepdims=True)
    return factor * grad_in - raw_vals * factor * factor * factor * inner_mean


def pair_cols(even, a, b):
    return jnp.where(even, a, b), jnp.where(even, b, a)


def rows_pair(even, mine, theirs):
    return jnp.where(even, jnp.concatenate([mine, theirs], 0), jnp.concatenate([theirs, mine], 0))


def nt(a, b):
    return lax.dot_general(a, b, (((1,), (1,)), ((), ())), preferred_element_type=f32)


def tn(a, b):
    return lax.dot_general(a, b, (((0,), (0,)), ((), ())), preferred_element_type=f32)


TILE = 896


def near():
    return pl.BlockSpec(memory_space=pltpu.VMEM)


def limit(mib):
    return pltpu.CompilerParams(vmem_limit_bytes=mib << 20)


def term_kernel(n_ref, g_ref, keep_ref, send_ref, turned):
    turned[...] = g_ref[...].T

    @pl.loop(0, n_ref.shape[1] // TILE)
    def _(i):
        spot = pl.ds(pl.multiple_of(i * TILE, TILE), TILE)
        out = jnp.dot(turned[...], n_ref[:, spot], preferred_element_type=f32).astype(bf16).T
        keep_ref[spot, :] = out[:, :HEAD_DIM]
        send_ref[spot, :] = out[:, HEAD_DIM:]


def weight_terms(normed, pair):
    rows, width = normed.shape
    shape = jax.ShapeDtypeStruct((width, HEAD_DIM), bf16)
    return pl.pallas_call(
        term_kernel,
        in_specs=[near(), near()],
        out_specs=[near(), near()],
        out_shape=[shape, shape],
        scratch_shapes=[pltpu.VMEM((2 * HEAD_DIM, rows), bf16)],
        compiler_params=limit(8),
        name="weight_terms",
    )(normed, pair)


def tokens_kernel(own_ref, far_ref, ka_ref, kb_ref, qa_ref, qb_ref, fa_ref, fb_ref, o_ref, turned):
    hd = HEAD_DIM
    turned[: 4 * hd] = own_ref[...].T
    turned[4 * hd :] = far_ref[...].T

    @pl.loop(0, o_ref.shape[1] // TILE)
    def _(i):
        spot = pl.ds(pl.multiple_of(i * TILE, TILE), TILE)
        rows = jnp.concatenate(
            [ka_ref[spot, :], kb_ref[spot, :], qa_ref[spot, :], qb_ref[spot, :],
             fa_ref[spot, :hd], fb_ref[spot, :hd], fa_ref[spot, hd:], fb_ref[spot, hd:]], 1)
        acc = jnp.dot(rows, turned[...], preferred_element_type=f32)
        o_ref[:, spot] = acc.astype(bf16).T


def token_terms(own, far, narrow, wide):
    rows, cols = own.shape
    width = wide[0].shape[0]
    return pl.pallas_call(
        tokens_kernel,
        in_specs=[near()] * 8,
        out_specs=near(),
        out_shape=jax.ShapeDtypeStruct((rows, width), bf16),
        scratch_shapes=[pltpu.VMEM((2 * cols, rows), bf16)],
        compiler_params=limit(12),
        name="token_terms",
    )(own, far, *narrow, *wide)


Q_TILE = 256


def attend_kernel(pos_ref, power_ref, q_ref, two_ref, one_ref, own_ref, cot_ref,
                  out_ref, gq_ref, two_out, one_out, own_out, ext, acc):
    hd = HEAD_DIM
    rows = own_ref.shape[0]
    step = pl.program_id(0)
    start = pl.multiple_of((step // 2) * Q_TILE, Q_TILE)
    span = ATTEND_SPAN + Q_TILE
    scale = float(ATTN_SCALAR) ** (-0.5)

    @pl.when(step == 0)
    def _():
        ext[:rows] = two_ref[...]
        ext[rows : 2 * rows] = one_ref[...]
        ext[2 * rows :] = own_ref[...]
        acc[...] = jnp.zeros_like(acc)

    q_raw = q_ref[...]
    factor = lax.rsqrt(jnp.mean(q_raw * q_raw, axis=1, keepdims=True) + norm_eps)
    queries = (q_raw * factor).astype(bf16)
    keys = ext[pl.ds(start, span), :hd]
    values = ext[pl.ds(start, span), hd:]
    scores = nt(queries, keys) * scale
    spot = lax.broadcasted_iota(jnp.int32, scores.shape, 1)
    gap = lax.broadcasted_iota(jnp.int32, scores.shape, 0) + ATTEND_SPAN - spot
    first = ATTEND_SPAN - pos_ref[0] * rows - start
    allowed = (gap >= 0) & (gap < ATTEND_SPAN) & (spot >= first)
    kernel = jnp.where(allowed, jnp.exp(scores), 0.0)
    totals = jnp.sum(kernel, axis=1, keepdims=True)
    probs = (kernel / totals).astype(bf16)
    mixed = jnp.dot(probs, values, preferred_element_type=f32)
    out_ref[...] = mixed.astype(bf16)
    grad_out = (cot_ref[...].astype(f32) * power_ref[0]).astype(bf16)
    delta = jnp.sum(grad_out.astype(f32) * mixed, axis=1, keepdims=True)
    grad_probs = nt(grad_out, values)
    grad_scores = (probs.astype(f32) * (grad_probs - delta) * scale).astype(bf16)
    grad_q = jnp.dot(grad_scores, keys, preferred_element_type=f32)
    inner = jnp.mean(q_raw * grad_q, axis=1, keepdims=True)
    gq_ref[...] = (factor * grad_q - q_raw * factor * factor * factor * inner).astype(bf16)
    acc[pl.ds(start, span), :hd] += tn(grad_scores, queries)
    acc[pl.ds(start, span), hd:] += tn(probs, grad_out)

    @pl.when(step == pl.num_programs(0) - 1)
    def _():
        two_out[...] = acc[:rows].astype(bf16)
        one_out[...] = acc[rows : 2 * rows].astype(bf16)
        own_out[...] = acc[2 * rows :]


def attend(pos, power, q_cols, two, one, own, cotangent):
    rows = own.shape[0]
    hd = HEAD_DIM
    whole = pl.BlockSpec((rows, 2 * hd), lambda i, p: (0, 0))
    plain = pl.BlockSpec((Q_TILE, hd), lambda i, p: (i // 2, i % 2))
    turned = pl.BlockSpec((Q_TILE, hd), lambda i, p: (i // 2, (i + p[1]) % 2))
    shape = lambda kind: jax.ShapeDtypeStruct((rows, 2 * hd), kind)
    return pl.pallas_call(
        attend_kernel,
        grid_spec=pltpu.PrefetchScalarGridSpec(
            num_scalar_prefetch=1,
            grid=(2 * rows // Q_TILE,),
            in_specs=[pl.BlockSpec(memory_space=pltpu.SMEM), turned, whole, whole, whole, plain],
            out_specs=[plain, turned, whole, whole, whole],
            scratch_shapes=[
                pltpu.VMEM((ATTEND_SPAN + rows, 2 * hd), bf16),
                pltpu.VMEM((ATTEND_SPAN + rows, 2 * hd), f32),
            ],
        ),
        out_shape=[shape(bf16), shape(bf16), shape(bf16), shape(bf16), shape(f32)],
        compiler_params=limit(24),
        name="attend",
    )(pos, power, q_cols, two, one, own, cotangent)


def step_kernel(info_ref, power_ref, mine_ref, got_ref, master_ref, first_ref, second_ref,
                master_out, first_out, second_out, grads):
    hd = HEAD_DIM
    rows = mine_ref.shape[0]
    even = info_ref[0] == 0
    for k, col in enumerate((1, 1, 0, 0)):
        mine = mine_ref[:, col * hd : (col + 1) * hd]
        got = got_ref[:, col * hd : (col + 1) * hd]
        grads[pl.ds(k, rows, stride=4), :] = jnp.where(even == (k % 2 == 0), mine, got)
    gradient = grads[...] / power_ref[0]
    master, first, second = master_ref[...], first_ref[...], second_ref[...]
    first_new = beta_one * first + (1.0 - beta_one) * gradient
    second_new = beta_two * second + (1.0 - beta_two) * gradient * gradient
    first_fix = 1.0 - beta_one**ADAM_STEP
    second_fix = 1.0 - beta_two**ADAM_STEP
    update = first_new / first_fix / (jnp.sqrt(second_new / second_fix) + adam_eps)
    applied = info_ref[1] == 0
    master_out[...] = jnp.where(
        applied, master - learn_rate * (update + weight_decay * master), master
    )
    first_out[...] = jnp.where(applied, first_new, first)
    second_out[...] = jnp.where(applied, second_new, second)


def adam_step(info, power, mine, got, master, first, second):
    smem = pl.BlockSpec(memory_space=pltpu.SMEM)
    return pl.pallas_call(
        step_kernel,
        in_specs=[smem, smem] + [near()] * 5,
        out_specs=[near()] * 3,
        out_shape=[jax.ShapeDtypeStruct(master.shape, f32)] * 3,
        scratch_shapes=[pltpu.VMEM(master.shape, f32)],
        compiler_params=limit(8),
        name="adam_step",
    )(info, power, mine, got, master, first, second)


def per_device(normed, cotangent, qkv_master, adam_first, adam_second, skip_flag, scale_exponent):
    tok_rows = normed.shape[0]
    hd = HEAD_DIM
    own_rows = qkv_master.shape[0]
    seq_pos = lax.axis_index("seq")
    head_pos = lax.axis_index("head")
    x, z, core = seq_pos // 8, (seq_pos // 2) % 4, seq_pos % 2
    half = head_pos // 4
    even = core == 0

    master16 = qkv_master.reshape(own_rows, 4 * hd).astype(bf16)
    cols = [master16[:, i * hd : (i + 1) * hd] for i in range(4)]
    kv_mine, kv_theirs = pair_cols(even, cols[2], cols[3])
    q_mine, q_theirs = pair_cols(even, cols[0], cols[1])
    got = swap_cores(jnp.concatenate([kv_theirs, q_theirs], 1))
    kv_block = rows_pair(even, kv_mine, got[:, :hd])
    q_block = rows_pair(even, q_mine, got[:, hd:])
    kv_q_block = jnp.concatenate([kv_block, q_block], 1)
    plane = gather_z(kv_q_block, z)
    kv_plane, q_plane = plane[:, :hd], plane[:, hd:]
    kv_parts = spread_x(kv_plane)
    q_parts = spread_x(tie(q_plane, kv_plane))
    far_block = head_move(tie(kv_q_block, plane), flip=True)
    kv_weights = join_x(kv_plane, kv_parts, x)
    kv_other = swap_cores(kv_weights)
    far_plane = gather_z(tie(far_block, kv_weights), z)

    kv = jnp.dot(normed, jnp.concatenate([kv_weights, kv_other], 1), preferred_element_type=f32)
    k_raw, v_raw = pair_cols(even, kv[:, :hd], kv[:, hd:])
    k_unit, k_factor = head_norm(k_raw)
    kv16 = jnp.concatenate([k_unit.astype(bf16), v_raw.astype(bf16)], 1)
    kv_two, kv_one = shifted(kv16, 2), shifted(kv16, 1)

    q_parts = list(lax.optimization_barrier((kv16, *q_parts))[1:])
    q_weights = join_x(q_plane, q_parts, x)
    q_other = swap_cores(q_weights)
    far_plane = tie(far_plane, q_weights)
    far_parts = spread_x(far_plane)

    q_cols = jnp.dot(normed, jnp.concatenate([q_weights, q_other], 1), preferred_element_type=f32)
    scale_power = jnp.left_shift(jnp.int32(1), scale_exponent).astype(f32)
    attn_out, gq_pair, part_two, part_one, part_own = attend(
        jnp.stack([seq_pos, core]), scale_power, tie(q_cols, far_plane),
        kv_two, kv_one, kv16, cotangent,
    )
    back_two, back_one = shifted(part_two, -2), shifted(part_one, -1)

    def weight_sum(pair):
        keep, send = weight_terms(normed, pair)
        got = swap_cores(send)
        return (keep.astype(f32) + got.astype(f32)).astype(bf16)

    move_x = lambda b, k: seq_move(b, dx=k)
    wq_sum = weight_sum(gq_pair)
    wq_parts = send_parts(wq_sum, x, move_x)

    grad_kv = part_own + back_one.astype(f32) + back_two.astype(f32)
    g_k = norm_back(k_raw, k_factor, grad_kv[:, :hd]).astype(bf16)
    g_v = grad_kv[:, hd:].astype(bf16)
    gkv_pair = jnp.concatenate(pair_cols(even, g_k, g_v), 1)
    far_parts = list(lax.optimization_barrier((gkv_pair, *far_parts))[1:])
    far_weights = join_x(far_plane, far_parts, x)
    far_other = swap_cores(far_weights)
    wkv_sum = weight_sum(gkv_pair)
    wkv_parts = send_parts(wkv_sum, x, move_x)

    g_all = jnp.concatenate([gkv_pair, gq_pair], 1)
    own_half = lax.dynamic_slice_in_dim(g_all, half * (tok_rows // 2), tok_rows // 2, 0)
    far_half = lax.dynamic_slice_in_dim(g_all, (1 - half) * (tok_rows // 2), tok_rows // 2, 0)
    got_half = head_move(far_half, flip=True)
    d_part = token_terms(
        own_half,
        got_half,
        (kv_weights, kv_other, q_weights, q_other),
        (far_weights, far_other),
    )
    d_blocks = lax.all_to_all(
        d_part.reshape(4, tok_rows // 8, -1), "head", split_axis=0, concat_axis=0, tiled=True,
        axis_index_groups=[[0, 1, 2, 3], [4, 5, 6, 7]],
    )
    d_tokens = add_parts([d_blocks[k] for k in range(4)]).astype(bf16)

    tied = lax.optimization_barrier((d_part, *wq_parts, *wkv_parts))[1:]
    w_x = jnp.concatenate(
        [add_parts(tied[4:]).astype(bf16), add_parts(tied[:4]).astype(bf16)], 1
    )
    z_parts = send_parts(w_x, z, lambda b, k: seq_move(b, dz=k))
    w_z = add_parts(z_parts)

    mine = lax.dynamic_slice_in_dim(w_z, core * own_rows, own_rows, 0)
    got = swap_cores(lax.dynamic_slice_in_dim(w_z, (1 - core) * own_rows, own_rows, 0))
    flag = lax.dynamic_index_in_dim(skip_flag, head_pos, 0, keepdims=False)
    flat = lambda a: a.reshape(own_rows * 4, hd)
    new = adam_step(
        jnp.stack([core, flag]), scale_power, mine, got,
        flat(qkv_master), flat(adam_first), flat(adam_second),
    )
    return (attn_out, d_tokens) + tuple(a.reshape(qkv_master.shape) for a in new)


def solution(mesh):
    return jax.shard_map(
        per_device,
        mesh=mesh,
        in_specs=(
            P("seq", None),
            P("seq", "head"),
            P("seq", "head", None),
            P("seq", "head", None),
            P("seq", "head", None),
            P(),
            P(),
        ),
        out_specs=(
            P("seq", "head"),
            P(("seq", "head"), None),
            P("seq", "head", None),
            P("seq", "head", None),
            P("seq", "head", None),
        ),
        check_vma=False,
    )
```

```python
import jax
import jax.numpy as jnp
from jax import lax
from jax.experimental import pallas as pl
from jax.experimental.pallas import tpu as pltpu
from jax.sharding import PartitionSpec as P

HEAD_DIM = 128
ATTEND_SPAN = 1024
ATTN_SCALAR = 168
ADAM_STEP = 1000

norm_eps = 1e-06
beta_one = 0.9
beta_two = 0.95
adam_eps = 1e-08
learn_rate = 0.01
weight_decay = 0.1

bf16 = jnp.bfloat16
f32 = jnp.float32

SEQ = 32
HEAD = 8


def seq_move(block, dx=0, dz=0, swap=False):
    pairs = []
    for s in range(SEQ):
        x, z, c = s // 8, (s // 2) % 4, s % 2
        pairs.append((s, ((x + dx) % 4) * 8 + ((z + dz) % 4) * 2 + (c ^ int(swap))))
    return lax.ppermute(block, "seq", pairs)


def head_move(block, dy=0, flip=False):
    pairs = []
    for h in range(HEAD):
        half, y = h // 4, h % 4
        pairs.append((h, (half ^ int(flip)) * 4 + (y + dy) % 4))
    return lax.ppermute(block, "head", pairs)


def swap_cores(block):
    return seq_move(block, swap=True)


def shifted(block, distance):
    route = [(i - distance, i) for i in range(SEQ) if 0 <= i - distance < SEQ]
    return lax.ppermute(block, "seq", route)


def tie(later, *earlier):
    return lax.optimization_barrier((later,) + earlier)[0]


def place(blocks, spots):
    out = jnp.broadcast_to(blocks[0][None], (4,) + blocks[0].shape)
    for block, spot in zip(blocks[1:], spots[1:]):
        out = lax.dynamic_update_slice(out, block[None], (spot,) + (0,) * block.ndim)
    return out.reshape((-1,) + blocks[0].shape[1:])


def gather_z(block, z):
    parts = [block] + [seq_move(block, dz=k) for k in (1, 2, 3)]
    return place(parts, [(z - k) % 4 for k in range(4)])


def spread_x(block):
    return [seq_move(block, dx=k) for k in (1, 3, 2)]


def join_x(block, parts, x):
    return place([block] + parts, [x, (x - 1) % 4, (x + 1) % 4, (x + 2) % 4])


def send_parts(total, pos, move):
    blocks = total.reshape(4, -1, total.shape[1])
    pick = lambda k: lax.dynamic_index_in_dim(blocks, (pos + k) % 4, 0, keepdims=False)
    return [pick(0)] + [move(pick(k), k) for k in (1, 3, 2)]


def add_parts(parts):
    return sum(p.astype(f32) for p in parts[1:]) + parts[0].astype(f32)


def head_norm(raw_vals):
    factor = lax.rsqrt(jnp.mean(raw_vals * raw_vals, axis=-1, keepdims=True) + norm_eps)
    return (raw_vals * factor, factor)


def norm_back(raw_vals, factor, grad_in):
    inner_mean = jnp.mean(raw_vals * grad_in, axis=-1, keepdims=True)
    return factor * grad_in - raw_vals * factor * factor * factor * inner_mean


def pair_cols(even, a, b):
    return jnp.where(even, a, b), jnp.where(even, b, a)


def rows_pair(even, mine, theirs):
    return jnp.where(even, jnp.concatenate([mine, theirs], 0), jnp.concatenate([theirs, mine], 0))


def nt(a, b):
    return lax.dot_general(a, b, (((1,), (1,)), ((), ())), preferred_element_type=f32)


def tn(a, b):
    return lax.dot_general(a, b, (((0,), (0,)), ((), ())), preferred_element_type=f32)


TILE = 896


def near():
    return pl.BlockSpec(memory_space=pltpu.VMEM)


def far_off():
    return pl.BlockSpec(memory_space=pltpu.HBM)


def limit(mib):
    return pltpu.CompilerParams(vmem_limit_bytes=mib << 20)


def term_kernel(n_ref, g_ref, keep_ref, send_ref, turned, held, sems):
    tiles = n_ref.shape[1] // TILE

    def tile(i):
        return pl.ds(pl.multiple_of(i * TILE, TILE), TILE)

    def copy(i):
        return pltpu.make_async_copy(n_ref.at[:, tile(i)], held.at[:, tile(i)], sems.at[i])

    @pl.loop(0, tiles)
    def _(i):
        copy(i).start()

    turned[...] = g_ref[...].T

    @pl.loop(0, tiles)
    def _(i):
        copy(i).wait()
        out = jnp.dot(turned[...], held[:, tile(i)], preferred_element_type=f32).astype(bf16).T
        keep_ref[tile(i), :] = out[:, :HEAD_DIM]
        send_ref[tile(i), :] = out[:, HEAD_DIM:]


def weight_terms(normed, pair):
    rows, width = normed.shape
    shape = jax.ShapeDtypeStruct((width, HEAD_DIM), bf16)
    return pl.pallas_call(
        term_kernel,
        in_specs=[far_off(), near()],
        out_specs=[near(), near()],
        out_shape=[shape, shape],
        scratch_shapes=[
            pltpu.VMEM((2 * HEAD_DIM, rows), bf16),
            pltpu.VMEM((rows, width), bf16),
            pltpu.SemaphoreType.DMA((width // TILE,)),
        ],
        compiler_params=limit(50),
        name="weight_terms",
    )(normed, pair)


def tokens_kernel(own_ref, far_ref, ka_ref, kb_ref, qa_ref, qb_ref, fa_ref, fb_ref, o_ref,
                  turned, rows, sems):
    hd = HEAD_DIM
    tiles = o_ref.shape[1] // TILE
    sources = ((ka_ref, 0), (kb_ref, 0), (qa_ref, 0), (qb_ref, 0),
               (fa_ref, 0), (fb_ref, 0), (fa_ref, hd), (fb_ref, hd))

    def tile(i):
        return pl.ds(pl.multiple_of(i * TILE, TILE), TILE)

    def copies(i):
        return [
            pltpu.make_async_copy(
                ref.at[tile(i), pl.ds(col, hd)], rows.at[tile(i), pl.ds(j * hd, hd)], sems.at[i, j]
            )
            for j, (ref, col) in enumerate(sources)
        ]

    @pl.loop(0, tiles)
    def _(i):
        for copy in copies(i):
            copy.start()

    turned[: 4 * hd] = own_ref[...].T
    turned[4 * hd :] = far_ref[...].T

    @pl.loop(0, tiles)
    def _(i):
        for copy in copies(i):
            copy.wait()
        acc = jnp.dot(rows[tile(i), :], turned[...], preferred_element_type=f32)
        o_ref[:, tile(i)] = acc.astype(bf16).T


def token_terms(own, far, narrow, wide):
    rows, cols = own.shape
    width = wide[0].shape[0]
    return pl.pallas_call(
        tokens_kernel,
        in_specs=[near(), near()] + [far_off()] * 4 + [pl.BlockSpec(memory_space=pl.ANY)] * 2,
        out_specs=near(),
        out_shape=jax.ShapeDtypeStruct((rows, width), bf16),
        scratch_shapes=[
            pltpu.VMEM((2 * cols, rows), bf16),
            pltpu.VMEM((width, 2 * cols), bf16),
            pltpu.SemaphoreType.DMA((width // TILE, 8)),
        ],
        compiler_params=limit(52),
        name="token_terms",
    )(own, far, *narrow, *wide)


Q_TILE = 256


def attend_kernel(pos_ref, power_ref, q_ref, two_ref, one_ref, own_ref, cot_ref,
                  out_ref, gq_ref, two_out, one_out, own_out, ext, acc):
    hd = HEAD_DIM
    rows = own_ref.shape[0]
    step = pl.program_id(0)
    start = pl.multiple_of((step // 2) * Q_TILE, Q_TILE)
    span = ATTEND_SPAN + Q_TILE
    scale = float(ATTN_SCALAR) ** (-0.5)

    @pl.when(step == 0)
    def _():
        ext[:rows] = two_ref[...]
        ext[rows : 2 * rows] = one_ref[...]
        ext[2 * rows :] = own_ref[...]
        acc[...] = jnp.zeros_like(acc)

    q_raw = q_ref[...]
    factor = lax.rsqrt(jnp.mean(q_raw * q_raw, axis=1, keepdims=True) + norm_eps)
    queries = (q_raw * factor).astype(bf16)
    keys = ext[pl.ds(start, span), :hd]
    values = ext[pl.ds(start, span), hd:]
    scores = nt(queries, keys) * scale
    spot = lax.broadcasted_iota(jnp.int32, scores.shape, 1)
    gap = lax.broadcasted_iota(jnp.int32, scores.shape, 0) + ATTEND_SPAN - spot
    first = ATTEND_SPAN - pos_ref[0] * rows - start
    allowed = (gap >= 0) & (gap < ATTEND_SPAN) & (spot >= first)
    kernel = jnp.where(allowed, jnp.exp(scores), 0.0)
    totals = jnp.sum(kernel, axis=1, keepdims=True)
    probs = (kernel / totals).astype(bf16)
    mixed = jnp.dot(probs, values, preferred_element_type=f32)
    out_ref[...] = mixed.astype(bf16)
    grad_out = (cot_ref[...].astype(f32) * power_ref[0]).astype(bf16)
    delta = jnp.sum(grad_out.astype(f32) * mixed, axis=1, keepdims=True)
    grad_probs = nt(grad_out, values)
    grad_scores = (probs.astype(f32) * (grad_probs - delta) * scale).astype(bf16)
    grad_q = jnp.dot(grad_scores, keys, preferred_element_type=f32)
    inner = jnp.mean(q_raw * grad_q, axis=1, keepdims=True)
    gq_ref[...] = (factor * grad_q - q_raw * factor * factor * factor * inner).astype(bf16)
    acc[pl.ds(start, span), :hd] += tn(grad_scores, queries)
    acc[pl.ds(start, span), hd:] += tn(probs, grad_out)

    @pl.when(step == pl.num_programs(0) - 1)
    def _():
        two_out[...] = acc[:rows].astype(bf16)
        one_out[...] = acc[rows : 2 * rows].astype(bf16)
        own_out[...] = acc[2 * rows :]


def attend(pos, power, q_cols, two, one, own, cotangent):
    rows = own.shape[0]
    hd = HEAD_DIM
    whole = pl.BlockSpec((rows, 2 * hd), lambda i, p: (0, 0))
    plain = pl.BlockSpec((Q_TILE, hd), lambda i, p: (i // 2, i % 2))
    turned = pl.BlockSpec((Q_TILE, hd), lambda i, p: (i // 2, (i + p[1]) % 2))
    shape = lambda kind: jax.ShapeDtypeStruct((rows, 2 * hd), kind)
    return pl.pallas_call(
        attend_kernel,
        grid_spec=pltpu.PrefetchScalarGridSpec(
            num_scalar_prefetch=1,
            grid=(2 * rows // Q_TILE,),
            in_specs=[pl.BlockSpec(memory_space=pltpu.SMEM), turned, whole, whole, whole, plain],
            out_specs=[plain, turned, whole, whole, whole],
            scratch_shapes=[
                pltpu.VMEM((ATTEND_SPAN + rows, 2 * hd), bf16),
                pltpu.VMEM((ATTEND_SPAN + rows, 2 * hd), f32),
            ],
        ),
        out_shape=[shape(bf16), shape(bf16), shape(bf16), shape(bf16), shape(f32)],
        compiler_params=limit(24),
        name="attend",
    )(pos, power, q_cols, two, one, own, cotangent)


def step_kernel(info_ref, power_ref, mine_ref, got_ref, master_ref, first_ref, second_ref,
                master_out, first_out, second_out, grads):
    hd = HEAD_DIM
    rows = mine_ref.shape[0]
    even = info_ref[0] == 0
    for k, col in enumerate((1, 1, 0, 0)):
        mine = mine_ref[:, col * hd : (col + 1) * hd]
        got = got_ref[:, col * hd : (col + 1) * hd]
        grads[pl.ds(k, rows, stride=4), :] = jnp.where(even == (k % 2 == 0), mine, got)
    gradient = grads[...] / power_ref[0]
    master, first, second = master_ref[...], first_ref[...], second_ref[...]
    first_new = beta_one * first + (1.0 - beta_one) * gradient
    second_new = beta_two * second + (1.0 - beta_two) * gradient * gradient
    first_fix = 1.0 - beta_one**ADAM_STEP
    second_fix = 1.0 - beta_two**ADAM_STEP
    update = first_new / first_fix / (jnp.sqrt(second_new / second_fix) + adam_eps)
    applied = info_ref[1] == 0
    master_out[...] = jnp.where(
        applied, master - learn_rate * (update + weight_decay * master), master
    )
    first_out[...] = jnp.where(applied, first_new, first)
    second_out[...] = jnp.where(applied, second_new, second)


def adam_step(info, power, mine, got, master, first, second):
    smem = pl.BlockSpec(memory_space=pltpu.SMEM)
    return pl.pallas_call(
        step_kernel,
        in_specs=[smem, smem] + [near()] * 5,
        out_specs=[near()] * 3,
        out_shape=[jax.ShapeDtypeStruct(master.shape, f32)] * 3,
        scratch_shapes=[pltpu.VMEM(master.shape, f32)],
        compiler_params=limit(8),
        name="adam_step",
    )(info, power, mine, got, master, first, second)


def per_device(normed, cotangent, qkv_master, adam_first, adam_second, skip_flag, scale_exponent):
    tok_rows = normed.shape[0]
    hd = HEAD_DIM
    own_rows = qkv_master.shape[0]
    seq_pos = lax.axis_index("seq")
    head_pos = lax.axis_index("head")
    x, z, core = seq_pos // 8, (seq_pos // 2) % 4, seq_pos % 2
    half = head_pos // 4
    even = core == 0

    master16 = qkv_master.reshape(own_rows, 4 * hd).astype(bf16)
    cols = [master16[:, i * hd : (i + 1) * hd] for i in range(4)]
    kv_mine, kv_theirs = pair_cols(even, cols[2], cols[3])
    q_mine, q_theirs = pair_cols(even, cols[0], cols[1])
    got = swap_cores(jnp.concatenate([kv_theirs, q_theirs], 1))
    kv_block = rows_pair(even, kv_mine, got[:, :hd])
    q_block = rows_pair(even, q_mine, got[:, hd:])
    kv_q_block = jnp.concatenate([kv_block, q_block], 1)
    plane = gather_z(kv_q_block, z)
    kv_plane, q_plane = plane[:, :hd], plane[:, hd:]
    kv_parts = spread_x(kv_plane)
    q_parts = spread_x(tie(q_plane, kv_plane))
    far_block = head_move(tie(kv_q_block, plane), flip=True)
    kv_weights = join_x(kv_plane, kv_parts, x)
    kv_other = swap_cores(kv_weights)
    far_plane = gather_z(tie(far_block, kv_weights), z)

    kv = jnp.dot(normed, jnp.concatenate([kv_weights, kv_other], 1), preferred_element_type=f32)
    k_raw, v_raw = pair_cols(even, kv[:, :hd], kv[:, hd:])
    k_unit, k_factor = head_norm(k_raw)
    kv16 = jnp.concatenate([k_unit.astype(bf16), v_raw.astype(bf16)], 1)
    kv_two, kv_one = shifted(kv16, 2), shifted(kv16, 1)

    q_parts = list(lax.optimization_barrier((kv16, *q_parts))[1:])
    q_weights = join_x(q_plane, q_parts, x)
    q_other = swap_cores(q_weights)
    far_plane = tie(far_plane, q_weights)
    far_parts = spread_x(far_plane)

    q_cols = jnp.dot(normed, jnp.concatenate([q_weights, q_other], 1), preferred_element_type=f32)
    scale_power = jnp.left_shift(jnp.int32(1), scale_exponent).astype(f32)
    attn_out, gq_pair, part_two, part_one, part_own = attend(
        jnp.stack([seq_pos, core]), scale_power, tie(q_cols, far_plane),
        kv_two, kv_one, kv16, cotangent,
    )
    back_two, back_one = shifted(part_two, -2), shifted(part_one, -1)

    def weight_sum(pair):
        keep, send = weight_terms(normed, pair)
        got = swap_cores(send)
        return (keep.astype(f32) + got.astype(f32)).astype(bf16)

    move_x = lambda b, k: seq_move(b, dx=k)
    wq_sum = weight_sum(gq_pair)
    wq_parts = send_parts(wq_sum, x, move_x)

    grad_kv = part_own + back_one.astype(f32) + back_two.astype(f32)
    g_k = norm_back(k_raw, k_factor, grad_kv[:, :hd]).astype(bf16)
    g_v = grad_kv[:, hd:].astype(bf16)
    gkv_pair = jnp.concatenate(pair_cols(even, g_k, g_v), 1)
    far_parts = list(lax.optimization_barrier((gkv_pair, *far_parts))[1:])
    far_weights = join_x(far_plane, far_parts, x)
    far_other = swap_cores(far_weights)
    wkv_sum = weight_sum(gkv_pair)
    wkv_parts = send_parts(wkv_sum, x, move_x)

    g_all = jnp.concatenate([gkv_pair, gq_pair], 1)
    own_half = lax.dynamic_slice_in_dim(g_all, half * (tok_rows // 2), tok_rows // 2, 0)
    far_half = lax.dynamic_slice_in_dim(g_all, (1 - half) * (tok_rows // 2), tok_rows // 2, 0)
    got_half = head_move(far_half, flip=True)
    d_part = token_terms(
        own_half,
        got_half,
        (kv_weights, kv_other, q_weights, q_other),
        (far_weights, far_other),
    )
    d_blocks = lax.all_to_all(
        d_part.reshape(4, tok_rows // 8, -1), "head", split_axis=0, concat_axis=0, tiled=True,
        axis_index_groups=[[0, 1, 2, 3], [4, 5, 6, 7]],
    )
    d_tokens = add_parts([d_blocks[k] for k in range(4)]).astype(bf16)

    tied = lax.optimization_barrier((d_part, *wq_parts, *wkv_parts))[1:]
    w_x = jnp.concatenate(
        [add_parts(tied[4:]).astype(bf16), add_parts(tied[:4]).astype(bf16)], 1
    )
    z_parts = send_parts(w_x, z, lambda b, k: seq_move(b, dz=k))
    w_z = add_parts(z_parts)

    mine = lax.dynamic_slice_in_dim(w_z, core * own_rows, own_rows, 0)
    got = swap_cores(lax.dynamic_slice_in_dim(w_z, (1 - core) * own_rows, own_rows, 0))
    flag = lax.dynamic_index_in_dim(skip_flag, head_pos, 0, keepdims=False)
    flat = lambda a: a.reshape(own_rows * 4, hd)
    new = adam_step(
        jnp.stack([core, flag]), scale_power, mine, got,
        flat(qkv_master), flat(adam_first), flat(adam_second),
    )
    return (attn_out, d_tokens) + tuple(a.reshape(qkv_master.shape) for a in new)


def solution(mesh):
    return jax.shard_map(
        per_device,
        mesh=mesh,
        in_specs=(
            P("seq", None),
            P("seq", "head"),
            P("seq", "head", None),
            P("seq", "head", None),
            P("seq", "head", None),
            P(),
            P(),
        ),
        out_specs=(
            P("seq", "head"),
            P(("seq", "head"), None),
            P("seq", "head", None),
            P("seq", "head", None),
            P("seq", "head", None),
        ),
        check_vma=False,
    )
```
